1024 devices in a mesh: blk: 64 (over x_lo, z, core), group: 16 (over y, x_hi).
Axes of the slice: x: 8 (x_hi: 2, x_lo: 4; x = x_hi * 4 + x_lo), y: 8, z: 8, core: 2. Of those that a mesh axis runs over, the one named last changes fastest.
Arguments:
- img_feat: bfloat16 [131072, 3072], P(('blk', 'group')), may hold values from -0.375 to 0.375
- head_weight: bfloat16 [3072, 512], replicated, may hold values from -1 to 3
- text_emb: bfloat16 [131072, 512], P(('blk', 'group')), may hold values from -0.375 to 0.375
- natural_exponent_factor: float32 [1], replicated, may hold values from 1.6 to 2
- bias: float32 [1], replicated, may hold values from -3.5 to -2.5
Outputs:
- d_feat: float32 [131072, 3072], P(('blk', 'group'))
- d_text: float32 [131072, 512], P(('blk', 'group'))
The draws below stay inside these ranges and needn't reach their ends.
All inputs are finite; a program needn't handle non-finite values.
Results may differ from the reference program's by a relative error of at most 0.005.
Values may be sent and summed in bfloat16 or wider, within the bound.
A program may use at most 32 MiB of HBM per device.

```python
import math
import jax
import jax.numpy as jnp
from jax import lax

EMB = 512
IMG_WIDTH = 3072
ROWS_DEV = 128
STEPS = 2
BATCH = 131072
N_BLK = 64
N_GROUP = 16


def shared_rows(key):
    base = jax.random.fold_in(key, 7101)
    centres = jax.random.normal(jax.random.fold_in(base, 1), (64, EMB), jnp.float32)
    first_ids = jax.random.randint(jax.random.fold_in(base, 2), (BATCH,), 0, 64)
    second_ids = jax.random.randint(jax.random.fold_in(base, 3), (BATCH,), 0, 64)
    first_coef = jax.random.normal(jax.random.fold_in(base, 4), (BATCH, 1), jnp.float32)
    second_coef = jax.random.normal(jax.random.fold_in(base, 5), (BATCH, 1), jnp.float32)
    own_part = jax.random.normal(jax.random.fold_in(base, 6), (BATCH, EMB), jnp.float32)
    mixed = first_coef * jnp.take(centres, first_ids, axis=0) + second_coef * jnp.take(centres, second_ids, axis=0)
    return 0.5477 * mixed + 0.6325 * own_part


def noise_and_scales(key, rows, columns):
    noise = jnp.clip(jax.random.normal(jax.random.fold_in(key, 1), (rows, columns), jnp.float32), -6.0, 6.0)
    scales = jnp.ones((rows, 1), jnp.float32)
    return (noise, scales)


def draw_img_feat(key, part):
    latent = shared_rows(key)
    noise, scales = noise_and_scales(jax.random.fold_in(key, 7202), BATCH, IMG_WIDTH)
    leading = latent + 0.5 * noise[:, :EMB]
    values = jnp.concatenate([leading, noise[:, EMB:]], axis=1)
    return jnp.clip(0.03125 * scales * values, -0.375, 0.375).astype(jnp.bfloat16)


def draw_text_emb(key, part):
    latent = shared_rows(key)
    noise, scales = noise_and_scales(jax.random.fold_in(key, 7303), BATCH, EMB)
    values = latent + 1.2 * noise
    return jnp.clip(0.03125 * scales * values, -0.375, 0.375).astype(jnp.bfloat16)


def draw_head_weight(key, part):
    base = jax.random.fold_in(key, 7404)
    noise = jnp.clip(jax.random.normal(base, (IMG_WIDTH, EMB), jnp.float32), -4.0, 4.0)
    row_index = jax.lax.broadcasted_iota(jnp.int32, (IMG_WIDTH, EMB), 0)
    col_index = jax.lax.broadcasted_iota(jnp.int32, (IMG_WIDTH, EMB), 1)
    leading = jnp.where(row_index == col_index, 2.0, 0.0).astype(jnp.float32)
    values = leading + noise / math.sqrt(IMG_WIDTH)
    return jnp.clip(values, -1.0, 3.0).astype(jnp.bfloat16)


def setup_inputs(seed: int = 0) -> dict:
    keys = jax.random.split(jax.random.key(seed), 6)
    img_feat = draw_img_feat(jax.random.fold_in(keys[5], 71), 0)
    head_weight = draw_head_weight(jax.random.fold_in(keys[5], 71), 0)
    text_emb = draw_text_emb(jax.random.fold_in(keys[5], 71), 0)
    natural_exponent_factor = jnp.clip(jax.random.uniform(keys[3], (1,), jnp.float32, 1.6, 2.0), 1.6, 2.0)
    bias = jnp.clip(jax.random.uniform(keys[4], (1,), jnp.float32, -3.5, -2.5), -3.5, -2.5)
    return {"img_feat": img_feat, "head_weight": head_weight, "text_emb": text_emb, "natural_exponent_factor": natural_exponent_factor, "bias": bias}


EPS = 1e-06

def to_unit(values):
    inverse = lax.rsqrt(lax.optimization_barrier(jnp.sum(values * values, axis=-1, keepdims=True)) + EPS)
    return (values * inverse, inverse)

def unit_back(grad_in, unit_rows, inverse):
    return (grad_in - unit_rows * lax.optimization_barrier(jnp.sum(unit_rows * grad_in, axis=-1, keepdims=True))) * inverse

def reference(img_feat, head_weight, text_emb, natural_exponent_factor, bias):
    similarity_multiplier = jnp.exp(natural_exponent_factor[0])
    partner_offset = bias[0]
    projected = jnp.dot(img_feat, head_weight, preferred_element_type=jnp.float32)
    img_unit, img_inv = to_unit(projected)
    txt_unit, txt_inv = to_unit(text_emb.astype(jnp.float32))
    panel_rows = ROWS_DEV * N_GROUP
    img_blocks = img_unit.astype(jnp.bfloat16).reshape(N_BLK, panel_rows, EMB).astype(jnp.float32)
    txt_blocks = txt_unit.astype(jnp.bfloat16).reshape(N_BLK, panel_rows, EMB).astype(jnp.float32)
    row_ids = lax.broadcasted_iota(jnp.int32, (panel_rows, panel_rows), 0)
    col_ids = lax.broadcasted_iota(jnp.int32, (panel_rows, panel_rows), 1)
    diagonal_mask = jnp.where(row_ids == col_ids, 1.0, 0.0).astype(jnp.float32)
    grad_img = jnp.zeros((N_BLK, panel_rows, EMB), jnp.float32)
    grad_txt = jnp.zeros((N_BLK, panel_rows, EMB), jnp.float32)
    for loop_step in range(STEPS):
        rolled = jnp.roll(txt_blocks, loop_step, axis=0)
        positive = diagonal_mask if loop_step == 0 else jnp.zeros_like(diagonal_mask)

        def block_terms(pair):
            picture_solo_vector, caption_solo_vector = pair
            matched_similarity_matrix = similarity_multiplier * jnp.dot(picture_solo_vector, caption_solo_vector.T, precision=lax.Precision.HIGHEST) + partner_offset
            weights_low = (jax.nn.sigmoid(matched_similarity_matrix) - positive).astype(jnp.bfloat16)
            weights_low = lax.optimization_barrier(weights_low)
            factor_matrix_expanded = weights_low.astype(jnp.float32)
            picture_addend = similarity_multiplier * jnp.dot(factor_matrix_expanded, caption_solo_vector, precision=lax.Precision.HIGHEST)
            caption_addend = similarity_multiplier * jnp.dot(factor_matrix_expanded.T, picture_solo_vector, precision=lax.Precision.HIGHEST)
            return (picture_addend, caption_addend)
        img_terms, txt_terms = lax.map(block_terms, (img_blocks, rolled))
        grad_img = grad_img + img_terms
        grad_txt = grad_txt + jnp.roll(txt_terms, -loop_step, axis=0)
    grad_img = grad_img.reshape(N_BLK * panel_rows, EMB)
    grad_txt = grad_txt.reshape(N_BLK * panel_rows, EMB)
    img_back = unit_back(grad_img, img_unit, img_inv).astype(jnp.bfloat16)
    d_feat = lax.dot_general(img_back, head_weight, (((1,), (1,)), ((), ())), preferred_element_type=jnp.float32)
    d_text = unit_back(grad_txt, txt_unit, txt_inv)
    return (d_feat, d_text)
```

```python
import functools

import jax
import jax.numpy as jnp
from jax import lax
from jax.experimental import pallas as pl
from jax.experimental.pallas import tpu as pltpu
from jax.sharding import PartitionSpec as P

EPS = 1e-06
MESH = pl.DeviceIdType.MESH
N_Y = 8
N_BLK = 64
ROWS = 128
HALF = 64
EMB = 512
WIDTH = 3072
K_CHUNKS = 4
LAST = (((1,), (1,)), ((), ()))

NEAR = {7: 0, 1: 1, 6: 2, 2: 3, 5: 4, 3: 5, 4: 6, 0: 7}
FAR = {0: 8, 4: 9, 7: 10, 1: 11, 6: 12, 2: 13, 5: 14, 3: 15}


def rows_of(place, half=None):
    if half is None:
        return pl.ds(place * ROWS, ROWS)
    return pl.ds(place * ROWS + half * HALF, HALF)


def kernel(
    nef_ref, bias_ref, txt_ref, feat_hbm, head_hbm, back_ref, dtext_ref,
    feat, head, txts, imgs, img_unit, own_acc, swap_acc, txt_acc,
    swap_out, swap_in, txt_out, txt_in, load_sem, send_sem, recv_sem,
):
    group = lax.axis_index("group")
    blk = lax.axis_index("blk")
    y, xh = group // 2, lax.rem(group, 2)
    up = {"group": lax.rem(y + 1, N_Y) * 2 + xh, "blk": blk}
    down = {"group": lax.rem(y + N_Y - 1, N_Y) * 2 + xh, "blk": blk}
    across = {"group": y * 2 + (1 - xh), "blk": blk}
    flip_next = jnp.where(blk == N_BLK - 1, 1 - xh, xh)
    flip_prev = jnp.where(blk == 0, 1 - xh, xh)
    after = {"group": y * 2 + flip_next, "blk": lax.rem(blk + 1, N_BLK)}
    before = {"group": y * 2 + flip_prev, "blk": lax.rem(blk + N_BLK - 1, N_BLK)}

    barrier = pltpu.get_barrier_semaphore()
    for peer in (up, down, across, after, before):
        pl.semaphore_signal(barrier, inc=1, device_id=peer, device_id_type=MESH)

    depth = WIDTH // K_CHUNKS
    loads = []
    for k in range(K_CHUNKS):
        span = pl.ds(k * depth, depth)
        pair = (
            pltpu.make_async_copy(feat_hbm.at[:, span], feat.at[:, span], load_sem.at[2 * k]),
            pltpu.make_async_copy(head_hbm.at[span], head.at[span], load_sem.at[2 * k + 1]),
        )
        for copy in pair:
            copy.start()
        loads.append(pair)

    copies = []

    def send(src, dst, peer):
        i = len(copies)
        copy = pltpu.make_async_remote_copy(
            src_ref=src, dst_ref=dst, send_sem=send_sem.at[i], recv_sem=recv_sem.at[i],
            device_id=peer, device_id_type=MESH,
        )
        copy.start()
        copies.append(copy)
        return copy

    def ring_hop(buf, places, moved, step, halves=(0, 1)):
        for half in halves:
            for way, peer in ((-1, up), (1, down)):
                src = (way * step) % N_Y
                dst = (way * (step + 1)) % N_Y
                if step == 3 and half != (0 if way == -1 else 1):
                    continue
                if step:
                    moved[src, half].wait_recv()
                moved[dst, half] = send(
                    buf.at[rows_of(places[src], half)], buf.at[rows_of(places[dst], half)], peer
                )
        if step == 3:
            moved[5, 1].wait_recv()
            moved[3, 0].wait_recv()

    def hand_on(slot):
        handed[slot] = send(txts.at[rows_of(NEAR[slot])], txts.at[rows_of(FAR[slot])], after)

    txt_moved, img_moved, swp_moved, handed = {}, {}, {}, {}

    words = txt_ref[...].astype(jnp.float32)
    txt_inv = lax.rsqrt(jnp.sum(words * words, axis=-1, keepdims=True) + EPS)
    txts[rows_of(NEAR[0])] = (words * txt_inv).astype(jnp.bfloat16)

    scale = jnp.exp(jnp.full((1, 1), nef_ref[0], jnp.float32))
    half_scale = 0.5 * scale
    half_bias = 0.5 * bias_ref[0]

    pl.semaphore_wait(barrier, 5)
    ring_hop(txts, NEAR, txt_moved, 0)
    hand_on(0)

    projected = jnp.zeros((ROWS, EMB), jnp.float32)
    for k in range(K_CHUNKS):
        span = pl.ds(k * depth, depth)
        for copy in loads[k]:
            copy.wait()
        projected += jnp.dot(feat[:, span], head[span], preferred_element_type=jnp.float32)
    img_inv = lax.rsqrt(jnp.sum(projected * projected, axis=-1, keepdims=True) + EPS)
    unit = projected * img_inv
    img_unit[...] = unit
    imgs[rows_of(NEAR[0])] = unit.astype(jnp.bfloat16)

    swapped = send(imgs.at[rows_of(NEAR[0])], imgs.at[rows_of(FAR[0])], across)
    ring_hop(imgs, NEAR, img_moved, 0)

    def terms(left, buf, place, pieces, own=False):
        right = buf[pl.ds(place * ROWS, pieces * ROWS)]
        dots = lax.dot_general(left, right, LAST, preferred_element_type=jnp.float32)
        weight = 0.5 * jnp.tanh(half_scale * dots + half_bias) + 0.5
        if own:
            row = lax.broadcasted_iota(jnp.int32, weight.shape, 0)
            col = lax.broadcasted_iota(jnp.int32, weight.shape, 1)
            weight = jnp.where(col == row + (pieces - 1) * ROWS, weight - 1.0, weight)
        return jnp.dot(weight.astype(jnp.bfloat16), right, preferred_element_type=jnp.float32)

    def own_img():
        return imgs[rows_of(NEAR[0])]

    def both_imgs():
        return imgs[pl.ds(NEAR[0] * ROWS, 2 * ROWS)]

    def both_txts():
        return txts[pl.ds(NEAR[0] * ROWS, 2 * ROWS)]

    ring_hop(txts, NEAR, txt_moved, 1)
    hand_on(7)
    hand_on(1)
    own_acc[...] = terms(own_img(), txts, 0, 2)
    ring_hop(imgs, NEAR, img_moved, 1)
    ring_hop(txts, NEAR, txt_moved, 2)
    hand_on(6)
    hand_on(2)
    handed[0].wait_recv()
    txt_acc[...] = terms(both_txts(), imgs, 0, 2)
    own_acc[...] += terms(own_img(), txts, 2, 2)
    ring_hop(txts, NEAR, txt_moved, 3)
    hand_on(5)
    hand_on(3)
    own_acc[...] += terms(own_img(), txts, 4, 2)
    ring_hop(imgs, NEAR, img_moved, 2)
    txt_acc[...] += terms(both_txts(), imgs, 2, 2)
    txt_moved[4, 0].wait_recv()
    txt_moved[4, 1].wait_recv()
    hand_on(4)
    own_acc[...] += terms(own_img(), txts, 6, 2, own=True)

    swapped.wait_recv()
    ring_hop(imgs, FAR, swp_moved, 0)
    swap_img = imgs[rows_of(FAR[0])]
    swap_acc[...] = terms(swap_img, txts, 0, 4)
    swap_acc[...] += terms(swap_img, txts, 4, 4)
    ring_hop(imgs, NEAR, img_moved, 3)
    for a, b in ((0, 4), (7, 1), (6, 2), (5, 3)):
        handed[a].wait_recv() if a else None
        handed[b].wait_recv()
        both = terms(both_imgs(), txts, FAR[a], 2)
        own_acc[...] += both[:ROWS]
        swap_acc[...] += both[ROWS:]
    swap_out[...] = swap_acc[...].astype(jnp.bfloat16)
    returned = send(swap_out, swap_in, across)

    ring_hop(imgs, FAR, swp_moved, 1)
    txt_acc[...] += terms(both_txts(), imgs, 4, 2)
    img_moved[4, 0].wait_recv()
    img_moved[4, 1].wait_recv()
    txt_acc[...] += terms(both_txts(), imgs, 6, 2, own=True)
    txt_acc[...] += terms(both_txts(), imgs, 10, 2)
    ring_hop(imgs, FAR, swp_moved, 2)
    txt_acc[...] += terms(both_txts(), imgs, 12, 2)
    ring_hop(imgs, FAR, swp_moved, 3)
    txt_acc[...] += terms(both_txts(), imgs, 14, 2)
    swp_moved[4, 0].wait_recv()
    swp_moved[4, 1].wait_recv()
    txt_acc[...] += terms(both_txts(), imgs, 8, 2)
    txt_out[...] = txt_acc[ROWS:].astype(jnp.bfloat16)
    given = send(txt_out, txt_in, before)

    def back(grad, unit_rows, inverse):
        return (grad - unit_rows * jnp.sum(unit_rows * grad, axis=-1, keepdims=True)) * inverse

    returned.wait_recv()
    grad = scale * (own_acc[...] + swap_in[...].astype(jnp.float32))
    back_ref[...] = back(grad, img_unit[...], img_inv).astype(jnp.bfloat16)
    given.wait_recv()
    grad = scale * (txt_acc[:ROWS] + txt_in[...].astype(jnp.float32))
    words = txt_ref[...].astype(jnp.float32)
    dtext_ref[...] = back(grad, words * txt_inv, txt_inv)

    for copy in copies:
        copy.wait_send()


N_COPIES = 3 * 14 + 8 + 3


def body(img_feat, head_weight, text_emb, natural_exponent_factor, bias):
    smem = pl.BlockSpec(memory_space=pltpu.SMEM)
    vmem = pl.BlockSpec(memory_space=pltpu.VMEM)
    hbm = pl.BlockSpec(memory_space=pl.ANY)
    back, d_text = pl.pallas_call(
        kernel,
        out_shape=(
            jax.ShapeDtypeStruct((ROWS, EMB), jnp.bfloat16),
            jax.ShapeDtypeStruct((ROWS, EMB), jnp.float32),
        ),
        in_specs=[smem, smem, vmem, hbm, hbm],
        out_specs=(vmem, vmem),
        scratch_shapes=[
            pltpu.VMEM((ROWS, WIDTH), jnp.bfloat16),
            pltpu.VMEM((WIDTH, EMB), jnp.bfloat16),
            pltpu.VMEM((16 * ROWS, EMB), jnp.bfloat16),
            pltpu.VMEM((16 * ROWS, EMB), jnp.bfloat16),
            pltpu.VMEM((ROWS, EMB), jnp.float32),
            pltpu.VMEM((ROWS, EMB), jnp.float32),
            pltpu.VMEM((ROWS, EMB), jnp.float32),
            pltpu.VMEM((2 * ROWS, EMB), jnp.float32),
            pltpu.VMEM((ROWS, EMB), jnp.bfloat16),
            pltpu.VMEM((ROWS, EMB), jnp.bfloat16),
            pltpu.VMEM((ROWS, EMB), jnp.bfloat16),
            pltpu.VMEM((ROWS, EMB), jnp.bfloat16),
            pltpu.SemaphoreType.DMA((2 * K_CHUNKS,)),
            pltpu.SemaphoreType.DMA((N_COPIES,)),
            pltpu.SemaphoreType.DMA((N_COPIES,)),
        ],
        compiler_params=pltpu.CompilerParams(collective_id=0, has_side_effects=True, vmem_limit_bytes=40 * 2**20),
        name="contrast",
    )(natural_exponent_factor, bias, text_emb, img_feat, head_weight)
    d_feat = lax.dot_general(back, head_weight, LAST, preferred_element_type=jnp.float32)
    return (d_feat, d_text)


def solution(mesh):
    return jax.shard_map(
        body,
        mesh=mesh,
        in_specs=(P(("blk", "group"), None), P(), P(("blk", "group"), None), P(), P()),
        out_specs=(P(("blk", "group"), None), P(("blk", "group"), None)),
        check_vma=False,
    )
```

```python
import functools

import jax
import jax.numpy as jnp
from jax import lax
from jax.experimental import pallas as pl
from jax.experimental.pallas import tpu as pltpu
from jax.sharding import PartitionSpec as P

EPS = 1e-06
MESH = pl.DeviceIdType.MESH
N_Y = 8
N_BLK = 64
ROWS = 128
PARTS = 2
PART = 64
EMB = 512
WIDTH = 3072
K_CHUNKS = 4
LAST = (((1,), (1,)), ((), ()))

NEAR = {7: 0, 1: 1, 6: 2, 2: 3, 5: 4, 3: 5, 4: 6, 0: 7}
FAR = {0: 8, 4: 9, 7: 10, 1: 11, 6: 12, 2: 13, 5: 14, 3: 15}


def rows_of(place, part=None):
    if part is None:
        return pl.ds(place * ROWS, ROWS)
    return pl.ds(place * ROWS + part * PART, PART)


def kernel(
    nef_ref, bias_ref, txt_hbm, feat_hbm, head_hbm, dfeat_ref, dtext_ref,
    feat, head, txt_ref, txts, imgs, img_unit, img_acc, txt_acc,
    swap_out, swap_in, txt_out, txt_in, load_sem, send_sem, recv_sem,
):
    group = lax.axis_index("group")
    blk = lax.axis_index("blk")
    y, xh = group // 2, lax.rem(group, 2)
    up = {"group": lax.rem(y + 1, N_Y) * 2 + xh, "blk": blk}
    down = {"group": lax.rem(y + N_Y - 1, N_Y) * 2 + xh, "blk": blk}
    across = {"group": y * 2 + (1 - xh), "blk": blk}
    flip_next = jnp.where(blk == N_BLK - 1, 1 - xh, xh)
    flip_prev = jnp.where(blk == 0, 1 - xh, xh)
    after = {"group": y * 2 + flip_next, "blk": lax.rem(blk + 1, N_BLK)}
    before = {"group": y * 2 + flip_prev, "blk": lax.rem(blk + N_BLK - 1, N_BLK)}

    barrier = pltpu.get_barrier_semaphore()
    for peer in (up, down, across, after, before):
        pl.semaphore_signal(barrier, inc=1, device_id=peer, device_id_type=MESH)

    text_load = pltpu.make_async_copy(txt_hbm, txt_ref, load_sem.at[2 * K_CHUNKS])
    text_load.start()
    depth = WIDTH // K_CHUNKS
    loads = []
    for k in range(K_CHUNKS):
        span = pl.ds(k * depth, depth)
        pair = (
            pltpu.make_async_copy(feat_hbm.at[:, span], feat.at[:, span], load_sem.at[2 * k]),
            pltpu.make_async_copy(head_hbm.at[span], head.at[span], load_sem.at[2 * k + 1]),
        )
        for copy in pair:
            copy.start()
        loads.append(pair)

    copies = []

    def send(src, dst, peer):
        i = len(copies)
        copy = pltpu.make_async_remote_copy(
            src_ref=src, dst_ref=dst, send_sem=send_sem.at[i], recv_sem=recv_sem.at[i],
            device_id=peer, device_id_type=MESH,
        )
        copy.start()
        copies.append(copy)
        return copy

    def ring_hop(buf, places, moved, step):
        for part in range(PARTS):
            for way, peer in ((-1, up), (1, down)):
                src = (way * step) % N_Y
                dst = (way * (step + 1)) % N_Y
                if step == 3 and (part < PARTS // 2) != (way == -1):
                    continue
                if step:
                    moved[src, part].wait_recv()
                moved[dst, part] = send(
                    buf.at[rows_of(places[src], part)], buf.at[rows_of(places[dst], part)], peer
                )
        if step == 3:
            for part in range(PARTS):
                moved[5 if part >= PARTS // 2 else 3, part].wait_recv()

    def ring_end(moved):
        for part in range(PARTS):
            moved[4, part].wait_recv()

    def hand_on(slot):
        handed[slot] = send(txts.at[rows_of(NEAR[slot])], txts.at[rows_of(FAR[slot])], after)

    txt_moved, img_moved, swp_moved, handed = {}, {}, {}, {}

    text_load.wait()
    words = txt_ref[...].astype(jnp.float32)
    txt_inv = lax.rsqrt(jnp.sum(words * words, axis=-1, keepdims=True) + EPS)
    txts[rows_of(NEAR[0])] = (words * txt_inv).astype(jnp.bfloat16)

    scale = jnp.exp(jnp.full((1, 1), nef_ref[0], jnp.float32))
    half_scale = 0.5 * scale
    half_bias = 0.5 * bias_ref[0]

    pl.semaphore_wait(barrier, 5)
    ring_hop(txts, NEAR, txt_moved, 0)
    hand_on(0)

    projected = jnp.zeros((ROWS, EMB), jnp.float32)
    for k in range(K_CHUNKS):
        span = pl.ds(k * depth, depth)
        for copy in loads[k]:
            copy.wait()
        projected += jnp.dot(feat[:, span], head[span], preferred_element_type=jnp.float32)
    img_inv = lax.rsqrt(jnp.sum(projected * projected, axis=-1, keepdims=True) + EPS)
    unit = projected * img_inv
    img_unit[...] = unit
    imgs[rows_of(NEAR[0])] = unit.astype(jnp.bfloat16)

    swapped = send(imgs.at[rows_of(NEAR[0])], imgs.at[rows_of(FAR[0])], across)
    ring_hop(imgs, NEAR, img_moved, 0)

    def terms(left, buf, place, pieces, own=False):
        right = buf[pl.ds(place * ROWS, pieces * ROWS)]
        dots = lax.dot_general(left, right, LAST, preferred_element_type=jnp.float32)
        weight = 0.5 * jnp.tanh(half_scale * dots + half_bias) + 0.5
        if own:
            row = lax.broadcasted_iota(jnp.int32, weight.shape, 0)
            col = lax.broadcasted_iota(jnp.int32, weight.shape, 1)
            weight = jnp.where(col == row + (pieces - 1) * ROWS, weight - 1.0, weight)
        return jnp.dot(weight.astype(jnp.bfloat16), right, preferred_element_type=jnp.float32)

    def both_imgs():
        return imgs[pl.ds(NEAR[0] * ROWS, 2 * ROWS)]

    def both_txts():
        return txts[pl.ds(NEAR[0] * ROWS, 2 * ROWS)]

    def add_img(place, own=False):
        img_acc[...] += terms(both_imgs(), txts, place, 2, own)

    def add_txt(place, own=False):
        txt_acc[...] += terms(both_txts(), imgs, place, 2, own)

    ring_hop(txts, NEAR, txt_moved, 1)
    hand_on(7)
    hand_on(1)
    ring_hop(imgs, NEAR, img_moved, 1)
    ring_hop(txts, NEAR, txt_moved, 2)
    hand_on(6)
    hand_on(2)
    swapped.wait_recv()
    ring_hop(imgs, FAR, swp_moved, 0)
    img_acc[...] = terms(both_imgs(), txts, 0, 2)
    ring_hop(txts, NEAR, txt_moved, 3)
    hand_on(5)
    hand_on(3)
    ring_hop(imgs, NEAR, img_moved, 2)
    add_img(2)
    ring_end(txt_moved)
    hand_on(4)
    ring_hop(imgs, FAR, swp_moved, 1)
    add_img(4)
    add_img(6, own=True)
    ring_hop(imgs, NEAR, img_moved, 3)
    for a, b in ((7, 1), (6, 2), (5, 3), (0, 4)):
        handed[a].wait_recv()
        handed[b].wait_recv()
        add_img(min(FAR[a], FAR[b]))
    swap_out[...] = img_acc[ROWS:].astype(jnp.bfloat16)
    returned = send(swap_out, swap_in, across)

    ring_hop(imgs, FAR, swp_moved, 2)
    txt_acc[...] = terms(both_txts(), imgs, 0, 2)
    add_txt(2)
    add_txt(4)
    ring_hop(imgs, FAR, swp_moved, 3)
    ring_end(img_moved)
    add_txt(6, own=True)
    add_txt(10)
    add_txt(12)
    add_txt(14)
    ring_end(swp_moved)
    add_txt(8)
    txt_out[...] = txt_acc[ROWS:].astype(jnp.bfloat16)
    given = send(txt_out, txt_in, before)

    def back(grad, unit_rows, inverse):
        return (grad - unit_rows * jnp.sum(unit_rows * grad, axis=-1, keepdims=True)) * inverse

    returned.wait_recv()
    grad = scale * (img_acc[:ROWS] + swap_in[...].astype(jnp.float32))
    img_back = back(grad, img_unit[...], img_inv).astype(jnp.bfloat16)
    for k in range(K_CHUNKS):
        span = pl.ds(k * depth, depth)
        dfeat_ref[:, span] = lax.dot_general(img_back, head[span], LAST, preferred_element_type=jnp.float32)
    given.wait_recv()
    grad = scale * (txt_acc[:ROWS] + txt_in[...].astype(jnp.float32))
    words = txt_ref[...].astype(jnp.float32)
    dtext_ref[...] = back(grad, words * txt_inv, txt_inv)

    for copy in copies:
        copy.wait_send()


N_COPIES = 3 * 7 * PARTS + 8 + 3


def body(img_feat, head_weight, text_emb, natural_exponent_factor, bias):
    smem = pl.BlockSpec(memory_space=pltpu.SMEM)
    vmem = pl.BlockSpec(memory_space=pltpu.VMEM)
    hbm = pl.BlockSpec(memory_space=pl.ANY)
    return pl.pallas_call(
        kernel,
        out_shape=(
            jax.ShapeDtypeStruct((ROWS, WIDTH), jnp.float32),
            jax.ShapeDtypeStruct((ROWS, EMB), jnp.float32),
        ),
        in_specs=[smem, smem, hbm, hbm, hbm],
        out_specs=(vmem, vmem),
        scratch_shapes=[
            pltpu.VMEM((ROWS, WIDTH), jnp.bfloat16),
            pltpu.VMEM((WIDTH, EMB), jnp.bfloat16),
            pltpu.VMEM((ROWS, EMB), jnp.bfloat16),
            pltpu.VMEM((16 * ROWS, EMB), jnp.bfloat16),
            pltpu.VMEM((16 * ROWS, EMB), jnp.bfloat16),
            pltpu.VMEM((ROWS, EMB), jnp.float32),
            pltpu.VMEM((2 * ROWS, EMB), jnp.float32),
            pltpu.VMEM((2 * ROWS, EMB), jnp.float32),
            pltpu.VMEM((ROWS, EMB), jnp.bfloat16),
            pltpu.VMEM((ROWS, EMB), jnp.bfloat16),
            pltpu.VMEM((ROWS, EMB), jnp.bfloat16),
            pltpu.VMEM((ROWS, EMB), jnp.bfloat16),
            pltpu.SemaphoreType.DMA((2 * K_CHUNKS + 1,)),
            pltpu.SemaphoreType.DMA((N_COPIES,)),
            pltpu.SemaphoreType.DMA((N_COPIES,)),
        ],
        compiler_params=pltpu.CompilerParams(collective_id=0, has_side_effects=True, vmem_limit_bytes=67043328),
        name="contrast",
    )(natural_exponent_factor, bias, text_emb, img_feat, head_weight)


def solution(mesh):
    return jax.shard_map(
        body,
        mesh=mesh,
        in_specs=(P(("blk", "group"), None), P(), P(("blk", "group"), None), P(), P()),
        out_specs=(P(("blk", "group"), None), P(("blk", "group"), None)),
        check_vma=False,
    )
```

```python
import functools

import jax
import jax.numpy as jnp
from jax import lax
from jax.experimental import pallas as pl
from jax.experimental.pallas import tpu as pltpu
from jax.sharding import PartitionSpec as P

EPS = 1e-06
MESH = pl.DeviceIdType.MESH
N_Y = 8
N_BLK = 64
ROWS = 128
PARTS = 2
PART = 64
EMB = 512
WIDTH = 3072
K_CHUNKS = 4
LAST = (((1,), (1,)), ((), ()))

NEAR = {7: 0, 1: 1, 6: 2, 2: 3, 5: 4, 3: 5, 4: 6, 0: 7}
FAR = {0: 8, 4: 9, 7: 10, 1: 11, 6: 12, 2: 13, 5: 14, 3: 15}


def rows_of(place, part=None):
    if part is None:
        return pl.ds(place * ROWS, ROWS)
    return pl.ds(place * ROWS + part * PART, PART)


def kernel(
    nef_ref, bias_ref, txt_hbm, feat_hbm, head_hbm, dfeat_ref, dtext_ref,
    feat, head, txt_ref, txts, imgs, img_unit, img_acc, txt_acc,
    swap_out, swap_in, txt_out, txt_in, load_sem, send_sem, recv_sem,
):
    group = lax.axis_index("group")
    blk = lax.axis_index("blk")
    y, xh = group // 2, lax.rem(group, 2)
    up = {"group": lax.rem(y + 1, N_Y) * 2 + xh, "blk": blk}
    down = {"group": lax.rem(y + N_Y - 1, N_Y) * 2 + xh, "blk": blk}
    across = {"group": y * 2 + (1 - xh), "blk": blk}
    flip_next = jnp.where(blk == N_BLK - 1, 1 - xh, xh)
    flip_prev = jnp.where(blk == 0, 1 - xh, xh)
    after = {"group": y * 2 + flip_next, "blk": lax.rem(blk + 1, N_BLK)}
    before = {"group": y * 2 + flip_prev, "blk": lax.rem(blk + N_BLK - 1, N_BLK)}

    barrier = pltpu.get_barrier_semaphore()
    for peer in (up, down, across, after, before):
        pl.semaphore_signal(barrier, inc=1, device_id=peer, device_id_type=MESH)

    text_load = pltpu.make_async_copy(txt_hbm, txt_ref, load_sem.at[2 * K_CHUNKS])
    text_load.start()
    depth = WIDTH // K_CHUNKS
    loads = []
    for k in range(K_CHUNKS):
        span = pl.ds(k * depth, depth)
        pair = (
            pltpu.make_async_copy(feat_hbm.at[:, span], feat.at[:, span], load_sem.at[2 * k]),
            pltpu.make_async_copy(head_hbm.at[span], head.at[span], load_sem.at[2 * k + 1]),
        )
        for copy in pair:
            copy.start()
        loads.append(pair)

    copies = []

    def send(src, dst, peer):
        i = len(copies)
        copy = pltpu.make_async_remote_copy(
            src_ref=src, dst_ref=dst, send_sem=send_sem.at[i], recv_sem=recv_sem.at[i],
            device_id=peer, device_id_type=MESH,
        )
        copy.start()
        copies.append(copy)
        return copy

    def ring_hop(buf, places, moved, step):
        for part in range(PARTS):
            for way, peer in ((-1, up), (1, down)):
                src = (way * step) % N_Y
                dst = (way * (step + 1)) % N_Y
                if step == 3 and (part < PARTS // 2) != (way == -1):
                    continue
                if step:
                    moved[src, part].wait_recv()
                moved[dst, part] = send(
                    buf.at[rows_of(places[src], part)], buf.at[rows_of(places[dst], part)], peer
                )
        if step == 3:
            for part in range(PARTS):
                moved[5 if part >= PARTS // 2 else 3, part].wait_recv()

    def ring_end(moved):
        for part in range(PARTS):
            moved[4, part].wait_recv()

    def hand_on(slot):
        handed[slot] = send(txts.at[rows_of(NEAR[slot])], txts.at[rows_of(FAR[slot])], after)

    txt_moved, img_moved, swp_moved, handed = {}, {}, {}, {}

    text_load.wait()
    words = txt_ref[...].astype(jnp.float32)
    txt_inv = lax.rsqrt(jnp.sum(words * words, axis=-1, keepdims=True) + EPS)
    txts[rows_of(NEAR[0])] = (words * txt_inv).astype(jnp.bfloat16)

    scale = jnp.exp(jnp.full((1, 1), nef_ref[0], jnp.float32))
    half_scale = 0.5 * scale
    half_bias = 0.5 * bias_ref[0]

    pl.semaphore_wait(barrier, 5)
    ring_hop(txts, NEAR, txt_moved, 0)
    hand_on(0)

    projected = jnp.zeros((ROWS, EMB), jnp.float32)
    for k in range(K_CHUNKS):
        span = pl.ds(k * depth, depth)
        for copy in loads[k]:
            copy.wait()
        projected += jnp.dot(feat[:, span], head[span], preferred_element_type=jnp.float32)
    img_inv = lax.rsqrt(jnp.sum(projected * projected, axis=-1, keepdims=True) + EPS)
    unit = projected * img_inv
    img_unit[...] = unit
    imgs[rows_of(NEAR[0])] = unit.astype(jnp.bfloat16)

    swapped = send(imgs.at[rows_of(NEAR[0])], imgs.at[rows_of(FAR[0])], across)
    ring_hop(imgs, NEAR, img_moved, 0)

    def terms(left, buf, place, pieces, own=False):
        right = buf[pl.ds(place * ROWS, pieces * ROWS)]
        dots = lax.dot_general(left, right, LAST, preferred_element_type=jnp.float32)
        weight = 0.5 * jnp.tanh(half_scale * dots + half_bias) + 0.5
        if own:
            row = lax.broadcasted_iota(jnp.int32, weight.shape, 0)
            col = lax.broadcasted_iota(jnp.int32, weight.shape, 1)
            weight = jnp.where(col == row + (pieces - 1) * ROWS, weight - 1.0, weight)
        return jnp.dot(weight.astype(jnp.bfloat16), right, preferred_element_type=jnp.float32)

    def both_imgs():
        return imgs[pl.ds(NEAR[0] * ROWS, 2 * ROWS)]

    def both_txts():
        return txts[pl.ds(NEAR[0] * ROWS, 2 * ROWS)]

    def add_img(place, own=False):
        img_acc[...] += terms(both_imgs(), txts, place, 2, own)

    def add_txt(place, own=False):
        txt_acc[...] += terms(both_txts(), imgs, place, 2, own)

    ring_hop(txts, NEAR, txt_moved, 1)
    hand_on(7)
    hand_on(1)
    ring_hop(imgs, NEAR, img_moved, 1)
    ring_hop(txts, NEAR, txt_moved, 2)
    hand_on(6)
    hand_on(2)
    swapped.wait_recv()
    ring_hop(imgs, FAR, swp_moved, 0)
    img_acc[...] = terms(both_imgs(), txts, 0, 2)
    ring_hop(txts, NEAR, txt_moved, 3)
    hand_on(5)
    hand_on(3)
    ring_hop(imgs, NEAR, img_moved, 2)
    add_img(2)
    ring_end(txt_moved)
    hand_on(4)
    ring_hop(imgs, FAR, swp_moved, 1)
    add_img(4)
    add_img(6, own=True)
    ring_hop(imgs, NEAR, img_moved, 3)
    ring_hop(imgs, FAR, swp_moved, 2)
    handed[7].wait_recv()
    handed[1].wait_recv()
    add_img(10)
    handed[6].wait_recv()
    handed[2].wait_recv()
    add_img(12)
    handed[5].wait_recv()
    handed[3].wait_recv()
    add_img(14)
    handed[0].wait_recv()
    handed[4].wait_recv()
    add_img(8)
    swap_out[...] = img_acc[ROWS:].astype(jnp.bfloat16)
    returned = send(swap_out, swap_in, across)
    ring_hop(imgs, FAR, swp_moved, 3)
    txt_acc[...] = terms(both_txts(), imgs, 0, 2)
    add_txt(2)
    add_txt(4)
    ring_end(img_moved)
    add_txt(6, own=True)
    add_txt(10)
    add_txt(12)
    add_txt(14)
    ring_end(swp_moved)
    add_txt(8)
    txt_out[...] = txt_acc[ROWS:].astype(jnp.bfloat16)
    given = send(txt_out, txt_in, before)

    def back(grad, unit_rows, inverse):
        return (grad - unit_rows * jnp.sum(unit_rows * grad, axis=-1, keepdims=True)) * inverse

    returned.wait_recv()
    grad = scale * (img_acc[:ROWS] + swap_in[...].astype(jnp.float32))
    img_back = back(grad, img_unit[...], img_inv).astype(jnp.bfloat16)
    for k in range(K_CHUNKS):
        span = pl.ds(k * depth, depth)
        dfeat_ref[:, span] = lax.dot_general(img_back, head[span], LAST, preferred_element_type=jnp.float32)
    given.wait_recv()
    grad = scale * (txt_acc[:ROWS] + txt_in[...].astype(jnp.float32))
    words = txt_ref[...].astype(jnp.float32)
    dtext_ref[...] = back(grad, words * txt_inv, txt_inv)

    for copy in copies:
        copy.wait_send()


N_COPIES = 3 * 7 * PARTS + 8 + 3


def body(img_feat, head_weight, text_emb, natural_exponent_factor, bias):
    smem = pl.BlockSpec(memory_space=pltpu.SMEM)
    vmem = pl.BlockSpec(memory_space=pltpu.VMEM)
    hbm = pl.BlockSpec(memory_space=pl.ANY)
    return pl.pallas_call(
        kernel,
        out_shape=(
            jax.ShapeDtypeStruct((ROWS, WIDTH), jnp.float32),
            jax.ShapeDtypeStruct((ROWS, EMB), jnp.float32),
        ),
        in_specs=[smem, smem, hbm, hbm, hbm],
        out_specs=(vmem, vmem),
        scratch_shapes=[
            pltpu.VMEM((ROWS, WIDTH), jnp.bfloat16),
            pltpu.VMEM((WIDTH, EMB), jnp.bfloat16),
            pltpu.VMEM((ROWS, EMB), jnp.bfloat16),
            pltpu.VMEM((16 * ROWS, EMB), jnp.bfloat16),
            pltpu.VMEM((16 * ROWS, EMB), jnp.bfloat16),
            pltpu.VMEM((ROWS, EMB), jnp.float32),
            pltpu.VMEM((2 * ROWS, EMB), jnp.float32),
            pltpu.VMEM((2 * ROWS, EMB), jnp.float32),
            pltpu.VMEM((ROWS, EMB), jnp.bfloat16),
            pltpu.VMEM((ROWS, EMB), jnp.bfloat16),
            pltpu.VMEM((ROWS, EMB), jnp.bfloat16),
            pltpu.VMEM((ROWS, EMB), jnp.bfloat16),
            pltpu.SemaphoreType.DMA((2 * K_CHUNKS + 1,)),
            pltpu.SemaphoreType.DMA((N_COPIES,)),
            pltpu.SemaphoreType.DMA((N_COPIES,)),
        ],
        compiler_params=pltpu.CompilerParams(collective_id=0, has_side_effects=True, vmem_limit_bytes=67043328),
        name="contrast",
    )(natural_exponent_factor, bias, text_emb, img_feat, head_weight)


def solution(mesh):
    return jax.shard_map(
        body,
        mesh=mesh,
        in_specs=(P(("blk", "group"), None), P(), P(("blk", "group"), None), P(), P()),
        out_specs=(P(("blk", "group"), None), P(("blk", "group"), None)),
        check_vma=False,
    )
```

```python
import functools

import jax
import jax.numpy as jnp
from jax import lax
from jax.experimental import pallas as pl
from jax.experimental.pallas import tpu as pltpu
from jax.sharding import PartitionSpec as P

EPS = 1e-06
MESH = pl.DeviceIdType.MESH
N_Y = 8
N_BLK = 64
ROWS = 128
PARTS = 2
PART = 64
EMB = 512
WIDTH = 3072
K_CHUNKS = 4
LAST = (((1,), (1,)), ((), ()))

NEAR = {7: 0, 1: 1, 6: 2, 2: 3, 5: 4, 3: 5, 4: 6, 0: 7}
FAR = {0: 8, 4: 9, 7: 10, 1: 11, 6: 12, 2: 13, 5: 14, 3: 15}


def rows_of(place, part=None):
    if part is None:
        return pl.ds(place * ROWS, ROWS)
    return pl.ds(place * ROWS + part * PART, PART)


def kernel(
    nef_ref, bias_ref, txt_hbm, feat_hbm, head_hbm, dfeat_hbm, dtext_ref,
    feat, head, txt_ref, dfeat, txts, imgs, img_unit, img_acc, txt_acc,
    swap_out, swap_in, txt_out, txt_in, load_sem, out_sem, send_sem, recv_sem,
):
    group = lax.axis_index("group")
    blk = lax.axis_index("blk")
    y, xh = group // 2, lax.rem(group, 2)
    up = {"group": lax.rem(y + 1, N_Y) * 2 + xh, "blk": blk}
    down = {"group": lax.rem(y + N_Y - 1, N_Y) * 2 + xh, "blk": blk}
    across = {"group": y * 2 + (1 - xh), "blk": blk}
    flip_next = jnp.where(blk == N_BLK - 1, 1 - xh, xh)
    flip_prev = jnp.where(blk == 0, 1 - xh, xh)
    after = {"group": y * 2 + flip_next, "blk": lax.rem(blk + 1, N_BLK)}
    before = {"group": y * 2 + flip_prev, "blk": lax.rem(blk + N_BLK - 1, N_BLK)}

    barrier = pltpu.get_barrier_semaphore()
    for peer in (up, down, across, after, before):
        pl.semaphore_signal(barrier, inc=1, device_id=peer, device_id_type=MESH)

    text_load = pltpu.make_async_copy(txt_hbm, txt_ref, load_sem.at[2 * K_CHUNKS])
    text_load.start()
    depth = WIDTH // K_CHUNKS
    loads = []
    for k in range(K_CHUNKS):
        span = pl.ds(k * depth, depth)
        pair = (
            pltpu.make_async_copy(feat_hbm.at[:, span], feat.at[:, span], load_sem.at[2 * k]),
            pltpu.make_async_copy(head_hbm.at[span], head.at[span], load_sem.at[2 * k + 1]),
        )
        for copy in pair:
            copy.start()
        loads.append(pair)

    copies = []

    def send(src, dst, peer):
        i = len(copies)
        copy = pltpu.make_async_remote_copy(
            src_ref=src, dst_ref=dst, send_sem=send_sem.at[i], recv_sem=recv_sem.at[i],
            device_id=peer, device_id_type=MESH,
        )
        copy.start()
        copies.append(copy)
        return copy

    def ring_hop(buf, places, moved, step):
        for part in range(PARTS):
            for way, peer in ((-1, up), (1, down)):
                src = (way * step) % N_Y
                dst = (way * (step + 1)) % N_Y
                if step == 3 and (part < PARTS // 2) != (way == -1):
                    continue
                if step or ((0, part) in moved and way == -1):
                    moved[src, part].wait_recv()
                moved[dst, part] = send(
                    buf.at[rows_of(places[src], part)], buf.at[rows_of(places[dst], part)], peer
                )
        if step == 3:
            for part in range(PARTS):
                moved[5 if part >= PARTS // 2 else 3, part].wait_recv()

    def ring_end(moved):
        for part in range(PARTS):
            moved[4, part].wait_recv()

    def hand_on(slot):
        handed[slot] = send(txts.at[rows_of(NEAR[slot])], txts.at[rows_of(FAR[slot])], after)

    txt_moved, img_moved, swp_moved, handed = {}, {}, {}, {}

    text_load.wait()
    words = txt_ref[...].astype(jnp.float32)
    txt_inv = lax.rsqrt(jnp.sum(words * words, axis=-1, keepdims=True) + EPS)
    txts[rows_of(NEAR[0])] = (words * txt_inv).astype(jnp.bfloat16)

    scale = jnp.exp(jnp.full((1, 1), nef_ref[0], jnp.float32))
    half_scale = 0.5 * scale
    half_bias = 0.5 * bias_ref[0]

    pl.semaphore_wait(barrier, 5)
    ring_hop(txts, NEAR, txt_moved, 0)
    hand_on(0)

    projected = jnp.zeros((ROWS, EMB), jnp.float32)
    for k in range(K_CHUNKS):
        span = pl.ds(k * depth, depth)
        for copy in loads[k]:
            copy.wait()
        projected += jnp.dot(feat[:, span], head[span], preferred_element_type=jnp.float32)
    img_inv = lax.rsqrt(jnp.sum(projected * projected, axis=-1, keepdims=True) + EPS)
    unit = projected * img_inv
    img_unit[...] = unit
    imgs[rows_of(NEAR[0])] = unit.astype(jnp.bfloat16)

    for part in range(PARTS):
        swp_moved[0, part] = send(
            imgs.at[rows_of(NEAR[0], part)], imgs.at[rows_of(FAR[0], part)], across
        )
    ring_hop(imgs, NEAR, img_moved, 0)

    def terms(left, buf, place, pieces, own=False):
        right = buf[pl.ds(place * ROWS, pieces * ROWS)]
        dots = lax.dot_general(left, right, LAST, preferred_element_type=jnp.float32)
        weight = 0.5 * jnp.tanh(half_scale * dots + half_bias) + 0.5
        if own:
            row = lax.broadcasted_iota(jnp.int32, weight.shape, 0)
            col = lax.broadcasted_iota(jnp.int32, weight.shape, 1)
            weight = jnp.where(col == row + (pieces - 1) * ROWS, weight - 1.0, weight)
        return jnp.dot(weight.astype(jnp.bfloat16), right, preferred_element_type=jnp.float32)

    def both_imgs():
        return imgs[pl.ds(NEAR[0] * ROWS, 2 * ROWS)]

    def both_txts():
        return txts[pl.ds(NEAR[0] * ROWS, 2 * ROWS)]

    def add_img(place, own=False):
        img_acc[...] += terms(both_imgs(), txts, place, 2, own)

    def add_txt(place, own=False):
        txt_acc[...] += terms(both_txts(), imgs, place, 2, own)

    ring_hop(txts, NEAR, txt_moved, 1)
    hand_on(7)
    hand_on(1)
    ring_hop(imgs, NEAR, img_moved, 1)
    ring_hop(txts, NEAR, txt_moved, 2)
    hand_on(6)
    hand_on(2)
    ring_hop(imgs, FAR, swp_moved, 0)
    img_acc[...] = terms(both_imgs(), txts, 0, 2)
    ring_hop(txts, NEAR, txt_moved, 3)
    hand_on(5)
    hand_on(3)
    ring_hop(imgs, NEAR, img_moved, 2)
    add_img(2)
    ring_end(txt_moved)
    hand_on(4)
    ring_hop(imgs, FAR, swp_moved, 1)
    add_img(4)
    add_img(6, own=True)
    ring_hop(imgs, NEAR, img_moved, 3)
    ring_hop(imgs, FAR, swp_moved, 2)
    handed[7].wait_recv()
    handed[1].wait_recv()
    add_img(10)
    handed[6].wait_recv()
    handed[2].wait_recv()
    add_img(12)
    handed[5].wait_recv()
    handed[3].wait_recv()
    add_img(14)
    handed[0].wait_recv()
    handed[4].wait_recv()
    add_img(8)
    swap_out[...] = img_acc[ROWS:].astype(jnp.bfloat16)
    returned = send(swap_out, swap_in, across)
    ring_hop(imgs, FAR, swp_moved, 3)
    txt_acc[...] = terms(both_txts(), imgs, 0, 2)
    add_txt(2)
    add_txt(4)
    ring_end(img_moved)
    add_txt(6, own=True)
    add_txt(10)
    add_txt(12)
    add_txt(14)
    ring_end(swp_moved)
    add_txt(8)
    txt_out[...] = txt_acc[ROWS:].astype(jnp.bfloat16)
    given = send(txt_out, txt_in, before)

    def back(grad, unit_rows, inverse):
        return (grad - unit_rows * jnp.sum(unit_rows * grad, axis=-1, keepdims=True)) * inverse

    returned.wait_recv()
    grad = scale * (img_acc[:ROWS] + swap_in[...].astype(jnp.float32))
    img_back = back(grad, img_unit[...], img_inv).astype(jnp.bfloat16)
    stores = []
    for k in range(K_CHUNKS):
        span = pl.ds(k * depth, depth)
        dfeat[:, span] = lax.dot_general(img_back, head[span], LAST, preferred_element_type=jnp.float32)
        stores.append(pltpu.make_async_copy(dfeat.at[:, span], dfeat_hbm.at[:, span], out_sem.at[k]))
        stores[k].start()
    given.wait_recv()
    grad = scale * (txt_acc[:ROWS] + txt_in[...].astype(jnp.float32))
    words = txt_ref[...].astype(jnp.float32)
    dtext_ref[...] = back(grad, words * txt_inv, txt_inv)

    for copy in stores:
        copy.wait()
    for copy in copies:
        copy.wait_send()


N_COPIES = 3 * 7 * PARTS + 8 + 2 + PARTS


def body(img_feat, head_weight, text_emb, natural_exponent_factor, bias):
    smem = pl.BlockSpec(memory_space=pltpu.SMEM)
    vmem = pl.BlockSpec(memory_space=pltpu.VMEM)
    hbm = pl.BlockSpec(memory_space=pl.ANY)
    return pl.pallas_call(
        kernel,
        out_shape=(
            jax.ShapeDtypeStruct((ROWS, WIDTH), jnp.float32),
            jax.ShapeDtypeStruct((ROWS, EMB), jnp.float32),
        ),
        in_specs=[smem, smem, hbm, hbm, hbm],
        out_specs=(hbm, vmem),
        scratch_shapes=[
            pltpu.VMEM((ROWS, WIDTH), jnp.bfloat16),
            pltpu.VMEM((WIDTH, EMB), jnp.bfloat16),
            pltpu.VMEM((ROWS, EMB), jnp.bfloat16),
            pltpu.VMEM((ROWS, WIDTH), jnp.float32),
            pltpu.VMEM((16 * ROWS, EMB), jnp.bfloat16),
            pltpu.VMEM((16 * ROWS, EMB), jnp.bfloat16),
            pltpu.VMEM((ROWS, EMB), jnp.float32),
            pltpu.VMEM((2 * ROWS, EMB), jnp.float32),
            pltpu.VMEM((2 * ROWS, EMB), jnp.float32),
            pltpu.VMEM((ROWS, EMB), jnp.bfloat16),
            pltpu.VMEM((ROWS, EMB), jnp.bfloat16),
            pltpu.VMEM((ROWS, EMB), jnp.bfloat16),
            pltpu.VMEM((ROWS, EMB), jnp.bfloat16),
            pltpu.SemaphoreType.DMA((2 * K_CHUNKS + 1,)),
            pltpu.SemaphoreType.DMA((K_CHUNKS,)),
            pltpu.SemaphoreType.DMA((N_COPIES,)),
            pltpu.SemaphoreType.DMA((N_COPIES,)),
        ],
        compiler_params=pltpu.CompilerParams(collective_id=0, has_side_effects=True, vmem_limit_bytes=67043328),
        name="contrast",
    )(natural_exponent_factor, bias, text_emb, img_feat, head_weight)


def solution(mesh):
    return jax.shard_map(
        body,
        mesh=mesh,
        in_specs=(P(("blk", "group"), None), P(), P(("blk", "group"), None), P(), P()),
        out_specs=(P(("blk", "group"), None), P(("blk", "group"), None)),
        check_vma=False,
    )
```

```python
import functools

import jax
import jax.numpy as jnp
from jax import lax
from jax.experimental import pallas as pl
from jax.experimental.pallas import tpu as pltpu
from jax.sharding import PartitionSpec as P

EPS = 1e-06
MESH = pl.DeviceIdType.MESH
N_Y = 8
N_BLK = 64
ROWS = 128
PARTS = 2
PART = 64
EMB = 512
WIDTH = 3072
K_CHUNKS = 4
LAST = (((1,), (1,)), ((), ()))

NEAR = {7: 0, 1: 1, 6: 2, 2: 3, 5: 4, 3: 5, 4: 6, 0: 7}
FAR = {0: 8, 4: 9, 7: 10, 1: 11, 6: 12, 2: 13, 5: 14, 3: 15}


def rows_of(place, part=None):
    if part is None:
        return pl.ds(place * ROWS, ROWS)
    return pl.ds(place * ROWS + part * PART, PART)


def kernel(
    nef_ref, bias_ref, txt_hbm, feat_hbm, head_hbm, dfeat_ref, dtext_ref,
    feat, head, txt_ref, txts, imgs, img_unit, img_acc, txt_acc,
    swap_out, swap_in, txt_out, txt_in, load_sem, send_sem, recv_sem,
):
    group = lax.axis_index("group")
    blk = lax.axis_index("blk")
    y, xh = group // 2, lax.rem(group, 2)
    up = {"group": lax.rem(y + 1, N_Y) * 2 + xh, "blk": blk}
    down = {"group": lax.rem(y + N_Y - 1, N_Y) * 2 + xh, "blk": blk}
    across = {"group": y * 2 + (1 - xh), "blk": blk}
    flip_next = jnp.where(blk == N_BLK - 1, 1 - xh, xh)
    flip_prev = jnp.where(blk == 0, 1 - xh, xh)
    after = {"group": y * 2 + flip_next, "blk": lax.rem(blk + 1, N_BLK)}
    before = {"group": y * 2 + flip_prev, "blk": lax.rem(blk + N_BLK - 1, N_BLK)}

    barrier = pltpu.get_barrier_semaphore()
    for peer in (up, down, across, after, before):
        pl.semaphore_signal(barrier, inc=1, device_id=peer, device_id_type=MESH)

    text_load = pltpu.make_async_copy(txt_hbm, txt_ref, load_sem.at[2 * K_CHUNKS])
    text_load.start()
    depth = WIDTH // K_CHUNKS
    loads = []
    for k in range(K_CHUNKS):
        span = pl.ds(k * depth, depth)
        pair = (
            pltpu.make_async_copy(feat_hbm.at[:, span], feat.at[:, span], load_sem.at[2 * k]),
            pltpu.make_async_copy(head_hbm.at[span], head.at[span], load_sem.at[2 * k + 1]),
        )
        for copy in pair:
            copy.start()
        loads.append(pair)

    copies = []

    def send(src, dst, peer):
        i = len(copies)
        copy = pltpu.make_async_remote_copy(
            src_ref=src, dst_ref=dst, send_sem=send_sem.at[i], recv_sem=recv_sem.at[i],
            device_id=peer, device_id_type=MESH,
        )
        copy.start()
        copies.append(copy)
        return copy

    def ring_hop(buf, places, moved, step):
        for part in range(PARTS):
            for way, peer in ((-1, up), (1, down)):
                src = (way * step) % N_Y
                dst = (way * (step + 1)) % N_Y
                if step == 3 and (part < PARTS // 2) != (way == -1):
                    continue
                if step or ((0, part) in moved and way == -1):
                    moved[src, part].wait_recv()
                moved[dst, part] = send(
                    buf.at[rows_of(places[src], part)], buf.at[rows_of(places[dst], part)], peer
                )
        if step == 3:
            for part in range(PARTS):
                moved[5 if part >= PARTS // 2 else 3, part].wait_recv()

    def ring_end(moved):
        for part in range(PARTS):
            moved[4, part].wait_recv()

    def hand_on(slot):
        handed[slot] = send(txts.at[rows_of(NEAR[slot])], txts.at[rows_of(FAR[slot])], after)

    txt_moved, img_moved, swp_moved, handed = {}, {}, {}, {}

    text_load.wait()
    words = txt_ref[...].astype(jnp.float32)
    txt_inv = lax.rsqrt(jnp.sum(words * words, axis=-1, keepdims=True) + EPS)
    txts[rows_of(NEAR[0])] = (words * txt_inv).astype(jnp.bfloat16)

    scale = jnp.exp(jnp.full((1, 1), nef_ref[0], jnp.float32))
    half_scale = 0.5 * scale
    half_bias = 0.5 * bias_ref[0]

    pl.semaphore_wait(barrier, 5)
    ring_hop(txts, NEAR, txt_moved, 0)
    hand_on(0)

    projected = jnp.zeros((ROWS, EMB), jnp.float32)
    for k in range(K_CHUNKS):
        span = pl.ds(k * depth, depth)
        for copy in loads[k]:
            copy.wait()
        projected += jnp.dot(feat[:, span], head[span], preferred_element_type=jnp.float32)
    img_inv = lax.rsqrt(jnp.sum(projected * projected, axis=-1, keepdims=True) + EPS)
    unit = projected * img_inv
    img_unit[...] = unit
    imgs[rows_of(NEAR[0])] = unit.astype(jnp.bfloat16)

    for part in range(PARTS):
        swp_moved[0, part] = send(
            imgs.at[rows_of(NEAR[0], part)], imgs.at[rows_of(FAR[0], part)], across
        )
    ring_hop(imgs, NEAR, img_moved, 0)

    def terms(left, buf, place, pieces, own=False):
        right = buf[pl.ds(place * ROWS, pieces * ROWS)]
        dots = lax.dot_general(left, right, LAST, preferred_element_type=jnp.float32)
        weight = 0.5 * jnp.tanh(half_scale * dots + half_bias) + 0.5
        if own:
            row = lax.broadcasted_iota(jnp.int32, weight.shape, 0)
            col = lax.broadcasted_iota(jnp.int32, weight.shape, 1)
            weight = jnp.where(col == row + (pieces - 1) * ROWS, weight - 1.0, weight)
        return jnp.dot(weight.astype(jnp.bfloat16), right, preferred_element_type=jnp.float32)

    def both_imgs():
        return imgs[pl.ds(NEAR[0] * ROWS, 2 * ROWS)]

    def both_txts():
        return txts[pl.ds(NEAR[0] * ROWS, 2 * ROWS)]

    def add_img(place, own=False):
        img_acc[...] += terms(both_imgs(), txts, place, 2, own)

    def add_txt(place, own=False):
        txt_acc[...] += terms(both_txts(), imgs, place, 2, own)

    ring_hop(txts, NEAR, txt_moved, 1)
    hand_on(7)
    hand_on(1)
    ring_hop(imgs, NEAR, img_moved, 1)
    ring_hop(txts, NEAR, txt_moved, 2)
    hand_on(6)
    hand_on(2)
    ring_hop(imgs, FAR, swp_moved, 0)
    img_acc[...] = terms(both_imgs(), txts, 0, 2)
    ring_hop(txts, NEAR, txt_moved, 3)
    hand_on(5)
    hand_on(3)
    ring_hop(imgs, NEAR, img_moved, 2)
    add_img(2)
    ring_end(txt_moved)
    hand_on(4)
    ring_hop(imgs, FAR, swp_moved, 1)
    add_img(4)
    add_img(6, own=True)
    ring_hop(imgs, NEAR, img_moved, 3)
    ring_hop(imgs, FAR, swp_moved, 2)
    handed[7].wait_recv()
    handed[1].wait_recv()
    add_img(10)
    handed[6].wait_recv()
    handed[2].wait_recv()
    add_img(12)
    handed[5].wait_recv()
    handed[3].wait_recv()
    add_img(14)
    handed[0].wait_recv()
    handed[4].wait_recv()
    add_img(8)
    swap_out[...] = img_acc[ROWS:].astype(jnp.bfloat16)
    returned = send(swap_out, swap_in, across)
    ring_hop(imgs, FAR, swp_moved, 3)
    txt_acc[...] = terms(both_txts(), imgs, 0, 2)
    add_txt(2)
    add_txt(4)
    ring_end(img_moved)
    add_txt(6, own=True)
    add_txt(10)
    add_txt(12)
    add_txt(14)
    ring_end(swp_moved)
    add_txt(8)
    txt_out[...] = txt_acc[ROWS:].astype(jnp.bfloat16)
    given = send(txt_out, txt_in, before)

    def back(grad, unit_rows, inverse):
        return (grad - unit_rows * jnp.sum(unit_rows * grad, axis=-1, keepdims=True)) * inverse

    returned.wait_recv()
    grad = scale * (img_acc[:ROWS] + swap_in[...].astype(jnp.float32))
    img_back = back(grad, img_unit[...], img_inv).astype(jnp.bfloat16)
    for k in range(K_CHUNKS):
        span = pl.ds(k * depth, depth)
        dfeat_ref[:, span] = lax.dot_general(img_back, head[span], LAST, preferred_element_type=jnp.float32)
    given.wait_recv()
    grad = scale * (txt_acc[:ROWS] + txt_in[...].astype(jnp.float32))
    words = txt_ref[...].astype(jnp.float32)
    dtext_ref[...] = back(grad, words * txt_inv, txt_inv)

    for copy in copies:
        copy.wait_send()


N_COPIES = 3 * 7 * PARTS + 8 + 2 + PARTS


def body(img_feat, head_weight, text_emb, natural_exponent_factor, bias):
    smem = pl.BlockSpec(memory_space=pltpu.SMEM)
    vmem = pl.BlockSpec(memory_space=pltpu.VMEM)
    hbm = pl.BlockSpec(memory_space=pl.ANY)
    return pl.pallas_call(
        kernel,
        out_shape=(
            jax.ShapeDtypeStruct((ROWS, WIDTH), jnp.float32),
            jax.ShapeDtypeStruct((ROWS, EMB), jnp.float32),
        ),
        in_specs=[smem, smem, hbm, hbm, hbm],
        out_specs=(vmem, vmem),
        scratch_shapes=[
            pltpu.VMEM((ROWS, WIDTH), jnp.bfloat16),
            pltpu.VMEM((WIDTH, EMB), jnp.bfloat16),
            pltpu.VMEM((ROWS, EMB), jnp.bfloat16),
            pltpu.VMEM((16 * ROWS, EMB), jnp.bfloat16),
            pltpu.VMEM((16 * ROWS, EMB), jnp.bfloat16),
            pltpu.VMEM((ROWS, EMB), jnp.float32),
            pltpu.VMEM((2 * ROWS, EMB), jnp.float32),
            pltpu.VMEM((2 * ROWS, EMB), jnp.float32),
            pltpu.VMEM((ROWS, EMB), jnp.bfloat16),
            pltpu.VMEM((ROWS, EMB), jnp.bfloat16),
            pltpu.VMEM((ROWS, EMB), jnp.bfloat16),
            pltpu.VMEM((ROWS, EMB), jnp.bfloat16),
            pltpu.SemaphoreType.DMA((2 * K_CHUNKS + 1,)),
            pltpu.SemaphoreType.DMA((N_COPIES,)),
            pltpu.SemaphoreType.DMA((N_COPIES,)),
        ],
        compiler_params=pltpu.CompilerParams(collective_id=0, has_side_effects=True, vmem_limit_bytes=50*2**20),
        name="contrast",
    )(natural_exponent_factor, bias, text_emb, img_feat, head_weight)


def solution(mesh):
    return jax.shard_map(
        body,
        mesh=mesh,
        in_specs=(P(("blk", "group"), None), P(), P(("blk", "group"), None), P(), P()),
        out_specs=(P(("blk", "group"), None), P(("blk", "group"), None)),
        check_vma=False,
    )
```
